32 devices in a mesh: dp: 2 (over core), seq: 4 (over y, x), head: 4 (over z).
Axes of the slice: x: 2, y: 2, z: 4, core: 2. Of those that a mesh axis runs over, the one named last changes fastest.
Arguments:
- query_rows: bfloat16 [2, 2048, 4096], P('dp', 'seq', 'head'), may hold values from -1.796875 to 1.796875
- key_rows: bfloat16 [2, 2048, 4096], P('dp', 'seq', 'head'), may hold values from -1.796875 to 1.796875
- value_rows: bfloat16 [2, 2048, 4096], P('dp', 'seq', 'head'), may hold values from -6 to 6
- norm_gain: float32 [4096], P('head'), may hold values from 0.1 to 1.9
- cotangent: bfloat16 [2, 2048, 4096], P('dp', 'seq', 'head'), may hold values from -10 to 10
- loss_mask: int32 [2, 2048], P('dp', 'seq'), may hold values 0 or 1
- importance: float32 [2, 2048], P('dp', 'seq'), may hold values from 0.5 to 2
- advantage: float32 [2], P('dp'), may hold values from -3 to 3
- lengths: int32 [2], P('dp'), may hold values from 512 to 2048, as said below
- decay_index: int32 [32], P('head'), may hold values from 0 to 11
Outputs:
- mixed: bfloat16 [2, 2048, 4096], P('dp', 'seq', 'head')
- query_grad: bfloat16 [2, 2048, 4096], P('dp', 'seq', 'head')
- key_grad: bfloat16 [2, 2048, 4096], P('dp', 'seq', 'head')
- value_grad: bfloat16 [2, 2048, 4096], P('dp', 'seq', 'head')
- gain_grad: float32 [4096], P('head')
The draws below stay inside these ranges and needn't reach their ends.
Inputs may be any that keep to these rules, and one draw needn't show every extreme that they name: `lengths`: at least one response has length 2048.
All inputs are finite; a program needn't handle non-finite values. No bound on the sum of `loss_mask` on one device may be relied on, other than what follows from the above.
Results may differ from the reference program's by a relative error of at most 0.0063.
Values sent between devices are 32-bit elements; how exact they have to be, the bound alone decides.
A program may use at most 128 MiB of HBM per device.

```python
import math
import jax
import jax.numpy as jnp
from jax import lax

HEAD_DIM = 128
TOK_DEV = 512
HEADS = 32
SEQ_LEN = 2048
BATCH = 2
N_SEQ = 4


def draw_cotangent(key, part):
    features = HEADS * HEAD_DIM
    order = jnp.arange(BATCH * SEQ_LEN, dtype=jnp.float32).reshape(BATCH, SEQ_LEN, 1)
    scale = 0.5 + order / (BATCH * SEQ_LEN - 1)
    base = jnp.clip(jax.random.normal(jax.random.fold_in(key, 13), (BATCH, SEQ_LEN, features), jnp.float32), -6.0, 6.0)
    values = base * scale
    return values.astype(jnp.bfloat16)


def draw_lengths(key, part):
    base = jax.random.randint(jax.random.fold_in(key, 21), (BATCH,), SEQ_LEN // 4, SEQ_LEN + 1, dtype=jnp.int32)
    chosen = jax.random.randint(jax.random.fold_in(key, 22), (), 0, BATCH, dtype=jnp.int32)
    rows = jnp.arange(BATCH, dtype=jnp.int32)
    return jnp.where(rows == chosen, jnp.int32(SEQ_LEN), base).astype(jnp.int32)


def place_ends(result, rng, smallest, largest):
    index_at = [jax.random.randint(jax.random.fold_in(rng, axis), (), 0, length) for axis, length in enumerate(result.shape)]
    main_axis = result.shape.index(max(result.shape))
    neighbour = index_at[:main_axis] + [(index_at[main_axis] + 1) % result.shape[main_axis]] + index_at[main_axis + 1:]
    return result.at[tuple(index_at)].set(smallest).at[tuple(neighbour)].set(largest)


def shard_levels(key, shape, split, least, top_value):
    def one(axis_at, blocks):
        steps = jax.random.uniform(jax.random.fold_in(jax.random.fold_in(key, 6), axis_at), (blocks,), jnp.float32, least / len(split), top_value / len(split))
        return jnp.repeat(jnp.exp(steps), shape[axis_at] // blocks).reshape((-1,) + (1,) * (len(shape) - axis_at - 1))

    factor_of = one(*split[0])
    for cut in split[1:]:
        factor_of = factor_of * one(*cut)
    return factor_of


def centred(stream_key, dims, scale, most, shards=(), held_as=jnp.bfloat16):
    loudness = shard_levels(stream_key, dims, shards, -0.22, 0.18) if shards else 1.0
    result = jax.random.normal(stream_key, dims, jnp.float32) * scale * loudness
    return jnp.minimum(jnp.maximum(result, -most), most).astype(held_as)


def setup_inputs(seed: int = 0) -> dict:
    streams_of = jax.random.split(jax.random.key(seed), 11)
    return {
        "query_rows": centred(streams_of[0], (BATCH, SEQ_LEN, HEADS * HEAD_DIM), 0.3, 1.796875, ((0, 2), (1, 4), (2, 4))),
        "key_rows": centred(streams_of[1], (BATCH, SEQ_LEN, HEADS * HEAD_DIM), 0.3, 1.796875, ((0, 2), (1, 4), (2, 4))),
        "value_rows": centred(streams_of[2], (BATCH, SEQ_LEN, HEADS * HEAD_DIM), 1.0, 6.0, ((0, 2), (1, 4), (2, 4))),
        "norm_gain": jnp.clip(1.0 + 0.18 * jax.random.normal(streams_of[3], (HEADS * HEAD_DIM,), jnp.float32), 0.1, 1.9),
        "cotangent": draw_cotangent(jax.random.fold_in(streams_of[10], 71), 0),
        "loss_mask": place_ends((jax.random.randint(streams_of[5], (BATCH, SEQ_LEN), 0, 4) < 3).astype(jnp.int32), jax.random.fold_in(streams_of[5], 1), 0, 1),
        "importance": jnp.clip(jnp.exp(math.log(2.0) - 1.3862944 * jax.random.uniform(streams_of[6], (BATCH, SEQ_LEN), jnp.float32) ** shard_levels(streams_of[6], (BATCH, SEQ_LEN), ((0, 2), (1, 4)), -0.2, 0.2)), 0.5, 2.0),
        "advantage": centred(streams_of[7], (BATCH,), 1.0, 3.0, ((0, 2),), jnp.float32),
        "lengths": draw_lengths(jax.random.fold_in(streams_of[10], 71), 0),
        "decay_index": place_ends(jax.random.randint(streams_of[9], (HEADS,), 0, 12), jax.random.fold_in(streams_of[9], 1), 0, 11).astype(jnp.int32),
    }


clip_high = 1.28
epsilon = 1e-06

def head_rates(decay_index):
    return 16.0 / (TOK_DEV * jnp.exp2(decay_index.astype(jnp.float32)))

def by_heads(array):
    return array.reshape(BATCH, N_SEQ, TOK_DEV, HEADS, HEAD_DIM).transpose(3, 0, 1, 2, 4)

def merge_heads(array):
    return array.transpose(1, 2, 3, 0, 4).reshape(BATCH, SEQ_LEN, HEADS * HEAD_DIM)

def decay_table(decay_rate):
    offsets = jnp.arange(TOK_DEV, dtype=jnp.float32)
    lagged = offsets[:, None] - offsets[None, :]
    within = jnp.where(lagged >= 0, jnp.exp2(-decay_rate * jnp.maximum(lagged, 0.0)), 0.0)
    return (offsets, within)

def carry_states(local_terms, factor, reverse):

    def advance(running, local_term):
        return (factor * running + local_term, running)
    zeros_state = jnp.zeros(local_terms.shape[1:], jnp.float32)
    _, passed = lax.scan(advance, zeros_state, local_terms, reverse=reverse)
    return passed

def forward_parts(queries, key_heads, value_heads, decay_rate):
    offsets, within = decay_table(decay_rate)
    scores = jnp.einsum('bntd,bnsd->bnts', queries.astype(jnp.float32), key_heads.astype(jnp.float32))
    score_half = (scores * within).astype(jnp.bfloat16)
    key_decayed = (key_heads.astype(jnp.float32) * jnp.exp2(-decay_rate * (TOK_DEV - 1 - offsets))[:, None]).astype(jnp.bfloat16)
    state_local = jnp.einsum('bntd,bnte->bnde', key_decayed.astype(jnp.float32), value_heads.astype(jnp.float32))
    passed = carry_states(state_local.transpose(1, 0, 2, 3), jnp.exp2(-decay_rate * TOK_DEV), False)
    state_half = passed.transpose(1, 0, 2, 3).astype(jnp.bfloat16)
    return (offsets, within, score_half, state_half)

def forward_head(queries, key_heads, value_heads, decay_rate):
    offsets, within, score_half, state_half = forward_parts(queries, key_heads, value_heads, decay_rate)
    local_out = jnp.einsum('bnts,bnse->bnte', score_half.astype(jnp.float32), value_heads.astype(jnp.float32))
    carried = jnp.einsum('bntd,bnde->bnte', queries.astype(jnp.float32), state_half.astype(jnp.float32))
    return local_out + carried * jnp.exp2(-decay_rate * (offsets + 1.0))[:, None]

def backward_head(queries, key_heads, value_heads, grad_heads, decay_rate):
    offsets, within, score_half, state_half = forward_parts(queries, key_heads, value_heads, decay_rate)
    f_query = queries.astype(jnp.float32)
    f_key = key_heads.astype(jnp.float32)
    f_value = value_heads.astype(jnp.float32)
    f_grad = grad_heads.astype(jnp.float32)
    dscore = (jnp.einsum('bnte,bnse->bnts', f_grad, f_value) * within).astype(jnp.bfloat16).astype(jnp.float32)
    query_decayed = (f_query * jnp.exp2(-decay_rate * offsets)[:, None]).astype(jnp.bfloat16)
    return_local = jnp.einsum('bntd,bnte->bnde', query_decayed.astype(jnp.float32), f_grad)
    passed = carry_states(return_local.transpose(1, 0, 2, 3), jnp.exp2(-decay_rate * TOK_DEV), True)
    return_half = passed.transpose(1, 0, 2, 3).astype(jnp.bfloat16).astype(jnp.float32)
    from_start = jnp.exp2(-decay_rate * (offsets + 1.0))[:, None]
    to_next = jnp.exp2(-decay_rate * (TOK_DEV - offsets))[:, None]
    query_grad = jnp.einsum('bnts,bnsd->bntd', dscore, f_key)
    query_grad = query_grad + jnp.einsum('bnte,bnde->bntd', f_grad, state_half.astype(jnp.float32)) * from_start
    key_grad = jnp.einsum('bnts,bntd->bnsd', dscore, f_query)
    key_grad = key_grad + jnp.einsum('bnte,bnde->bntd', f_value, return_half) * to_next
    value_grad = jnp.einsum('bnts,bnte->bnse', score_half.astype(jnp.float32), f_grad)
    value_grad = value_grad + jnp.einsum('bntd,bnde->bnte', f_key, return_half) * to_next
    return (query_grad, key_grad, value_grad)

def reference(query_rows, key_rows, value_rows, norm_gain, cotangent, loss_mask, importance, advantage, lengths, decay_index):
    decay_rates = head_rates(decay_index)
    query_heads = by_heads(query_rows)
    key_heads = by_heads(key_rows)
    value_heads = by_heads(value_rows)

    def forward_bundle(bundle):
        return forward_head(bundle[0], bundle[1], bundle[2], bundle[3])
    head_outs = lax.map(forward_bundle, (query_heads, key_heads, value_heads, decay_rates))
    outputs_flat = merge_heads(head_outs)
    features = HEADS * HEAD_DIM
    positions = jnp.arange(SEQ_LEN, dtype=jnp.int32)
    in_length = (positions[None, :] < lengths[:, None]).astype(jnp.float32)
    token_weight = loss_mask.astype(jnp.float32) * in_length * jnp.minimum(importance, clip_high)
    token_weight = token_weight * advantage[:, None] * (float(SEQ_LEN) / lengths.astype(jnp.float32))[:, None]
    grad_y = cotangent.astype(jnp.float32) * token_weight[..., None]
    grad_n = grad_y * norm_gain
    inverse = lax.rsqrt(lax.optimization_barrier(jnp.sum(outputs_flat * outputs_flat, -1)) / features + epsilon)
    normed = outputs_flat * inverse[..., None]
    mixed = (normed * norm_gain).astype(jnp.bfloat16)
    mean_term = lax.optimization_barrier(jnp.sum(grad_n * outputs_flat, -1)) * inverse / features
    grad_out = (inverse[..., None] * (grad_n - normed * mean_term[..., None])).astype(jnp.bfloat16)
    gain_grad = lax.optimization_barrier(jnp.sum(grad_y * normed, axis=(0, 1)))
    grad_heads = by_heads(grad_out)

    def backward_bundle(bundle):
        return backward_head(bundle[0], bundle[1], bundle[2], bundle[3], bundle[4])
    gradients = lax.map(backward_bundle, (query_heads, key_heads, value_heads, grad_heads, decay_rates))
    query_grad = merge_heads(gradients[0]).astype(jnp.bfloat16)
    key_grad = merge_heads(gradients[1]).astype(jnp.bfloat16)
    value_grad = merge_heads(gradients[2]).astype(jnp.bfloat16)
    return (mixed, query_grad, key_grad, value_grad, gain_grad)
```

```python
import functools

import jax
import jax.numpy as jnp
from jax import lax
from jax.experimental import pallas as pl
from jax.experimental.pallas import tpu as pltpu
from jax.sharding import PartitionSpec as P

clip_high = 1.28
epsilon = 1e-06
f32 = jnp.float32
bf16 = jnp.bfloat16
MESH = pl.DeviceIdType.MESH


def dot(a, b, ca, cb):
    return lax.dot_general(a, b, (((ca,), (cb,)), ((), ())), preferred_element_type=f32)


def kernel(
    n_seq,
    n_head,
    n_dp,
    decay_ref,
    adv_ref,
    len_ref,
    gain_ref,
    mask_ref,
    imp_ref,
    q_hbm,
    k_hbm,
    v_hbm,
    c_hbm,
    o_mix,
    o_dq,
    o_dk,
    o_dv,
    gg_ref,
    q,
    k,
    v,
    c,
    out,
    go,
    pk,
    pv,
    probs,
    wtab,
    tot_f,
    rcv_f,
    tot_b,
    rcv_b,
    pref,
    state,
    stat,
    gsum,
    grcv,
    in_sem,
    fs_sem,
    fr_sem,
    bs_sem,
    br_sem,
    ss_sem,
    sr_sem,
    gs_sem,
    gr_sem,
):
    slab, features = q.shape
    heads = decay_ref.shape[0]
    dim = features // heads
    blk = min(256, slab)
    nblk = slab // blk
    stages = n_seq.bit_length() - 1
    me = lax.axis_index("seq")
    mh = lax.axis_index("head")
    md = lax.axis_index("dp")

    def partner(step):
        g = 1 << step
        bit = lax.rem(lax.div(me, g), 2)
        return me + g * (1 - 2 * bit)

    loads = [
        pltpu.make_async_copy(src.at[0], dst, in_sem.at[i])
        for i, (src, dst) in enumerate(((k_hbm, k), (v_hbm, v), (q_hbm, q), (c_hbm, c)))
    ]
    for load in loads:
        load.start()

    barrier = pltpu.get_barrier_semaphore()
    for s in range(stages):
        pl.semaphore_signal(barrier, inc=1, device_id={"seq": partner(s)}, device_id_type=MESH)
    for off in range(1, n_head):
        pl.semaphore_signal(
            barrier, inc=1, device_id={"head": lax.rem(mh + off, n_head)}, device_id_type=MESH
        )
    for off in range(1, n_dp):
        pl.semaphore_signal(
            barrier, inc=1, device_id={"dp": lax.rem(md + off, n_dp)}, device_id_type=MESH
        )
    pl.semaphore_wait(barrier, stages + n_head - 1 + n_dp - 1)

    def cols(h):
        return pl.ds(pl.multiple_of(h * dim, dim), dim)

    def rate(h, width):
        index = jnp.full((1, width), decay_ref[h], jnp.int32).astype(f32)
        return 16.0 / (slab * jnp.exp2(index))

    def rows_at(width):
        return lax.broadcasted_iota(jnp.int32, (slab, width), 0).astype(f32)

    def fwd_copy(s, h):
        return pltpu.make_async_remote_copy(
            src_ref=tot_f.at[s, h],
            dst_ref=rcv_f.at[s, h],
            send_sem=fs_sem.at[s, h],
            recv_sem=fr_sem.at[s, h],
            device_id={"seq": partner(s)},
            device_id_type=MESH,
        )

    def bwd_copy(s, h):
        return pltpu.make_async_remote_copy(
            src_ref=tot_b.at[s, h],
            dst_ref=rcv_b.at[s, h],
            send_sem=bs_sem.at[s, h],
            recv_sem=br_sem.at[s, h],
            device_id={"seq": partner(s)},
            device_id_type=MESH,
        )

    def merge(h, s, place, tot, rcv, first):
        g = 1 << s
        r = rate(h, dim) * slab
        upper = jnp.full((1, dim), lax.rem(lax.div(place, g), 2), jnp.int32).astype(f32)
        inner = jnp.full((1, dim), lax.rem(place, g), jnp.int32).astype(f32)
        got = rcv[s, h]
        to_prefix = upper * jnp.exp2(-r * inner)
        if first:
            pref[h] = to_prefix * got
        else:
            pref[h] = pref[h] + to_prefix * got
        if s + 1 < stages:
            whole = jnp.exp2(-r * g)
            from_got = upper * whole + (1.0 - upper)
            from_own = upper + (1.0 - upper) * whole
            tot[s + 1, h] = from_got * got + from_own * tot[s, h]

    loads[0].wait()
    loads[1].wait()

    @pl.loop(0, heads)
    def _(h):
        fade = jnp.exp2(-rate(h, dim) * (slab - 1.0 - rows_at(dim)))
        faded = (k[:, cols(h)].astype(f32) * fade).astype(bf16)
        tot_f[0, h] = dot(faded, v[:, cols(h)], 0, 0)
        fwd_copy(0, h).start()

    loads[2].wait()

    t_at = lax.broadcasted_iota(jnp.int32, (blk, blk), 0)
    s_at = lax.broadcasted_iota(jnp.int32, (blk, blk), 1)

    @pl.loop(0, heads)
    def _(h):
        r = rate(h, blk)
        near = jnp.exp2(-r * (t_at - s_at).astype(f32))
        wtab[h, 0] = jnp.where(t_at >= s_at, near, 0.0)
        for d in range(1, nblk):
            wtab[h, d] = near * jnp.exp2(-r * float(blk * d))
        for i in range(nblk):
            rows = pl.ds(i * blk, blk)
            total = None
            for j in range(i + 1):
                past = pl.ds(j * blk, blk)
                score = dot(q[rows, cols(h)], k[past, cols(h)], 1, 1)
                half = (score * wtab[h, i - j]).astype(bf16)
                probs[h, rows, past] = half
                part = dot(half, v[past, cols(h)], 1, 0)
                total = part if total is None else total + part
            out[rows, cols(h)] = total
        fwd_copy(0, h).wait()
        merge(h, 0, me, tot_f, rcv_f, True)
        if stages > 1:
            fwd_copy(1, h).start()

    for s in range(1, stages - 1):

        @pl.loop(0, heads)
        def _(h, s=s):
            fwd_copy(s, h).wait()
            merge(h, s, me, tot_f, rcv_f, False)
            fwd_copy(s + 1, h).start()

    loads[3].wait()

    token = mask_ref[...].astype(f32)
    at = me * slab + lax.broadcasted_iota(jnp.int32, (1, slab), 1)
    length = jnp.full((1, slab), len_ref[0], jnp.int32)
    token = token * (at < length).astype(f32) * jnp.minimum(imp_ref[...], clip_high)
    token = token * adv_ref[0] * (float(slab * n_seq) / length.astype(f32))

    def finish(h, carry):
        squares, mixes = carry
        if stages > 1:
            fwd_copy(stages - 1, h).wait()
            merge(h, stages - 1, me, tot_f, rcv_f, False)
        half = pref[h].astype(bf16)
        state[h] = half
        grow = jnp.exp2(-rate(h, dim) * (rows_at(dim) + 1.0))
        full = out[:, cols(h)] + dot(q[:, cols(h)], half, 1, 0) * grow
        out[:, cols(h)] = full
        gain = gain_ref[pl.ds(h, 1), :]
        return squares + full * full, mixes + c[:, cols(h)].astype(f32) * gain * full

    zeros = jnp.zeros((slab, dim), f32)
    squares, mixes = lax.fori_loop(0, heads, finish, (zeros, zeros))
    stat[mh, 0:1, :] = jnp.sum(squares.T, axis=0, keepdims=True)
    stat[mh, 1:2, :] = jnp.sum(mixes.T, axis=0, keepdims=True) * token
    sends = [
        pltpu.make_async_remote_copy(
            src_ref=stat.at[mh],
            dst_ref=stat.at[mh],
            send_sem=ss_sem.at[off - 1],
            recv_sem=sr_sem.at[off - 1],
            device_id={"head": lax.rem(mh + off, n_head)},
            device_id_type=MESH,
        )
        for off in range(1, n_head)
    ]
    for send in sends:
        send.start()
    for send in sends:
        send.wait()
    sums = stat[0]
    for i in range(1, n_head):
        sums = sums + stat[i]
    count = features * n_head
    inverse = lax.rsqrt(sums[0:1] / count + epsilon)
    mean = inverse * (sums[1:2] / count)

    def column(row):
        return jnp.broadcast_to(row, (dim, slab)).T

    inv_col = column(inverse)
    give_col = column(inverse * token)
    take_col = column(inverse * inverse * mean)

    @pl.loop(0, heads)
    def _(h):
        gain = gain_ref[pl.ds(h, 1), :]
        full = out[:, cols(h)]
        given = c[:, cols(h)].astype(f32) * give_col
        o_mix[0, :, cols(h)] = (full * inv_col * gain).astype(bf16)
        gsum[0, pl.ds(h, 1), :] = jnp.sum(given * full, axis=0, keepdims=True)
        grad = (given * gain - take_col * full).astype(bf16)
        go[:, cols(h)] = grad
        fade = jnp.exp2(-rate(h, dim) * rows_at(dim))
        faded = (q[:, cols(h)].astype(f32) * fade).astype(bf16)
        tot_b[0, h] = dot(faded, grad, 0, 0)
        bwd_copy(0, h).start()

    def gain_copy(s):
        target = {"dp": lax.rem(md + 1, n_dp)} if s == stages else {"seq": partner(s)}
        return pltpu.make_async_remote_copy(
            src_ref=gsum.at[s],
            dst_ref=grcv.at[s],
            send_sem=gs_sem.at[s],
            recv_sem=gr_sem.at[s],
            device_id=target,
            device_id_type=MESH,
        )

    gain_copy(0).start()
    back = n_seq - 1 - me

    @pl.loop(0, heads)
    def _(h):
        for i in range(nblk):
            rows = pl.ds(i * blk, blk)
            grad = go[rows, cols(h)]
            qi = q[rows, cols(h)]
            total = None
            for j in range(i + 1):
                past = pl.ds(j * blk, blk)
                score = dot(grad, v[past, cols(h)], 1, 1)
                half = (score * wtab[h, i - j]).astype(bf16)
                part = dot(half, k[past, cols(h)], 1, 0)
                total = part if total is None else total + part
                dk = dot(half, qi, 0, 0)
                dv = dot(probs[h, rows, past], grad, 0, 0)
                if j == i:
                    pk[past, cols(h)] = dk
                    pv[past, cols(h)] = dv
                else:
                    pk[past, cols(h)] += dk
                    pv[past, cols(h)] += dv
            grow = jnp.exp2(-rate(h, dim) * (rows_at(dim)[i * blk : (i + 1) * blk] + 1.0))
            total = total + dot(grad, state[h], 1, 1) * grow
            o_dq[0, rows, cols(h)] = total.astype(bf16)
        bwd_copy(0, h).wait()
        merge(h, 0, back, tot_b, rcv_b, True)
        if stages > 1:
            bwd_copy(1, h).start()

    rounds = stages + (1 if n_dp > 1 else 0)
    for s in range(rounds):
        gain_copy(s).wait()
        gsum[s + 1] = gsum[s] + grcv[s]
        if s + 1 < rounds:
            gain_copy(s + 1).start()
    gg_ref[...] = gsum[rounds]

    for s in range(1, stages - 1):

        @pl.loop(0, heads)
        def _(h, s=s):
            bwd_copy(s, h).wait()
            merge(h, s, back, tot_b, rcv_b, False)
            bwd_copy(s + 1, h).start()

    @pl.loop(0, heads)
    def _(h):
        if stages > 1:
            bwd_copy(stages - 1, h).wait()
            merge(h, stages - 1, back, tot_b, rcv_b, False)
        half = pref[h].astype(bf16)
        fade = jnp.exp2(-rate(h, dim) * (slab - rows_at(dim)))
        dk = pk[:, cols(h)] + dot(v[:, cols(h)], half, 1, 1) * fade
        o_dk[0, :, cols(h)] = dk.astype(bf16)
        dv = pv[:, cols(h)] + dot(k[:, cols(h)], half, 1, 0) * fade
        o_dv[0, :, cols(h)] = dv.astype(bf16)


def on_device(
    n_seq,
    n_head,
    n_dp,
    query_rows,
    key_rows,
    value_rows,
    norm_gain,
    cotangent,
    loss_mask,
    importance,
    advantage,
    lengths,
    decay_index,
):
    batches, slab, features = query_rows.shape
    heads = decay_index.shape[0]
    dim = features // heads
    stages = n_seq.bit_length() - 1
    assert batches == 1 and n_seq == 1 << stages and stages > 0 and n_dp <= 2
    vmem = pl.BlockSpec(memory_space=pltpu.VMEM)
    smem = pl.BlockSpec(memory_space=pltpu.SMEM)
    far = pl.BlockSpec(memory_space=pltpu.HBM)
    rows = jax.ShapeDtypeStruct(query_rows.shape, bf16)
    wide = pltpu.VMEM((slab, features), bf16)
    wide32 = pltpu.VMEM((slab, features), f32)
    blk = min(256, slab)
    states = pltpu.VMEM((stages, heads, dim, dim), f32)
    dma = pltpu.SemaphoreType.DMA
    mixed, dq, dk, dv, gain_grad = pl.pallas_call(
        functools.partial(kernel, n_seq, n_head, n_dp),
        out_shape=(rows, rows, rows, rows, jax.ShapeDtypeStruct((heads, dim), f32)),
        in_specs=[smem] * 3 + [vmem] * 3 + [far] * 4,
        out_specs=(vmem,) * 5,
        scratch_shapes=[wide] * 4
        + [wide32, wide, wide32, wide32]
        + [
            pltpu.VMEM((heads, slab, slab), bf16),
            pltpu.VMEM((heads, slab // blk, blk, blk), f32),
            states,
            states,
            states,
            states,
            pltpu.VMEM((heads, dim, dim), f32),
            pltpu.VMEM((heads, dim, dim), bf16),
            pltpu.VMEM((n_head, 2, slab), f32),
            pltpu.VMEM((stages + 2, heads, dim), f32),
            pltpu.VMEM((stages + 1, heads, dim), f32),
            dma((4,)),
            dma((stages, heads)),
            dma((stages, heads)),
            dma((stages, heads)),
            dma((stages, heads)),
            dma((max(n_head - 1, 1),)),
            dma((max(n_head - 1, 1),)),
            dma((stages + 1,)),
            dma((stages + 1,)),
        ],
        compiler_params=pltpu.CompilerParams(
            collective_id=0, has_side_effects=True, vmem_limit_bytes=48 << 20
        ),
        name="lightning",
    )(
        decay_index,
        advantage,
        lengths,
        norm_gain.reshape(heads, dim),
        loss_mask,
        importance,
        query_rows,
        key_rows,
        value_rows,
        cotangent,
    )
    return (mixed, dq, dk, dv, gain_grad.reshape(features))


def solution(mesh):
    wide = P("dp", "seq", "head")
    token = P("dp", "seq")
    in_specs = (wide, wide, wide, P("head"), wide, token, token, P("dp"), P("dp"), P("head"))
    out_specs = (wide, wide, wide, wide, P("head"))
    body = functools.partial(on_device, mesh.shape["seq"], mesh.shape["head"], mesh.shape["dp"])
    return jax.shard_map(
        body, mesh=mesh, in_specs=in_specs, out_specs=out_specs, check_vma=False
    )
```

```python
import functools

import jax
import jax.numpy as jnp
from jax import lax
from jax.experimental import pallas as pl
from jax.experimental.pallas import tpu as pltpu
from jax.sharding import PartitionSpec as P

clip_high = 1.28
epsilon = 1e-06
f32 = jnp.float32
bf16 = jnp.bfloat16
MESH = pl.DeviceIdType.MESH


def dot(a, b, ca, cb):
    return lax.dot_general(a, b, (((ca,), (cb,)), ((), ())), preferred_element_type=f32)


def kernel(
    n_seq,
    n_head,
    n_dp,
    decay_hbm,
    adv_ref,
    len_ref,
    gain_hbm,
    mask_hbm,
    imp_hbm,
    q_hbm,
    k_hbm,
    v_hbm,
    c_hbm,
    o_mix,
    o_dq,
    o_dk,
    o_dv,
    gg_ref,
    decay_ref,
    gain_ref,
    mask_ref,
    imp_ref,
    q,
    k,
    v,
    c,
    out,
    go,
    pk,
    pv,
    probs,
    dsc,
    wtab,
    up,
    down,
    squares,
    mixes,
    tot_f,
    rcv_f,
    tot_b,
    rcv_b,
    pref,
    state,
    stat,
    gsum,
    grcv,
    in_sem,
    small_sem,
    fs_sem,
    fr_sem,
    bs_sem,
    br_sem,
    ss_sem,
    sr_sem,
    gs_sem,
    gr_sem,
):
    slab, features = q.shape
    heads = decay_ref.shape[0]
    dim = features // heads
    blk = min(256, slab)
    nblk = slab // blk
    stages = n_seq.bit_length() - 1
    me = lax.axis_index("seq")
    mh = lax.axis_index("head")
    md = lax.axis_index("dp")

    def partner(step):
        g = 1 << step
        bit = lax.rem(lax.div(me, g), 2)
        return me + g * (1 - 2 * bit)

    loads = [
        pltpu.make_async_copy(src.at[0], dst, in_sem.at[i])
        for i, (src, dst) in enumerate(((k_hbm, k), (v_hbm, v), (q_hbm, q), (c_hbm, c)))
    ]
    small = [
        pltpu.make_async_copy(src, dst, small_sem.at[i])
        for i, (src, dst) in enumerate(
            (
                (decay_hbm, decay_ref),
                (gain_hbm, gain_ref),
                (mask_hbm, mask_ref),
                (imp_hbm, imp_ref),
            )
        )
    ]
    for load in small + loads:
        load.start()

    barrier = pltpu.get_barrier_semaphore()
    for s in range(stages):
        pl.semaphore_signal(barrier, inc=1, device_id={"seq": partner(s)}, device_id_type=MESH)
    for off in range(1, n_head):
        pl.semaphore_signal(
            barrier, inc=1, device_id={"head": lax.rem(mh + off, n_head)}, device_id_type=MESH
        )
    for off in range(1, n_dp):
        pl.semaphore_signal(
            barrier, inc=1, device_id={"dp": lax.rem(md + off, n_dp)}, device_id_type=MESH
        )

    def cols(h):
        return pl.ds(pl.multiple_of(h * dim, dim), dim)

    def rate(h, width):
        index = jnp.full((1, width), decay_ref[h], jnp.int32).astype(f32)
        return 16.0 / (slab * jnp.exp2(index))

    small[0].wait()
    base = min(128, slab)
    line = lax.broadcasted_iota(jnp.int32, (base, dim), 0).astype(f32)

    @pl.loop(0, heads)
    def _(h):
        r = rate(h, dim)
        rise = jnp.exp2(-r * line)
        fall = jnp.exp2(-r * (base - 1.0 - line))
        for b in range(slab // base):
            rows = pl.ds(b * base, base)
            up[h, rows, :] = rise * jnp.exp2(-r * float(b * base))
            down[h, rows, :] = fall * jnp.exp2(-r * float(slab - (b + 1) * base))

    pl.semaphore_wait(barrier, stages + n_head - 1 + n_dp - 1)

    def fwd_copy(s, h):
        return pltpu.make_async_remote_copy(
            src_ref=tot_f.at[s, h],
            dst_ref=rcv_f.at[s, h],
            send_sem=fs_sem.at[s, h],
            recv_sem=fr_sem.at[s, h],
            device_id={"seq": partner(s)},
            device_id_type=MESH,
        )

    def bwd_copy(s, h):
        return pltpu.make_async_remote_copy(
            src_ref=tot_b.at[s, h],
            dst_ref=rcv_b.at[s, h],
            send_sem=bs_sem.at[s, h],
            recv_sem=br_sem.at[s, h],
            device_id={"seq": partner(s)},
            device_id_type=MESH,
        )

    def lower_only(s, place):
        return lax.div(place, 2 << s) == n_seq // (2 << s) - 1

    def is_upper(s, place):
        return lax.rem(lax.div(place, 1 << s), 2) == 1

    def sends(s, place):
        return jnp.logical_not(jnp.logical_and(is_upper(s, place), lower_only(s, place)))

    def takes(s, place):
        return jnp.logical_or(is_upper(s, place), jnp.logical_not(lower_only(s, place)))

    def begin(copy, s, h, place):
        @pl.when(sends(s, place))
        def _():
            copy(s, h).start()

    def settle(copy, place):
        for s in range(stages):

            @pl.when(sends(s, place))
            def _(s=s):
                @pl.loop(0, heads)
                def _(h):
                    copy(s, h).wait_send()

    def accept(copy, h, s, place, tot, rcv):
        first = s == 0
        if first:

            @pl.when(jnp.logical_not(takes(s, place)))
            def _():
                pref[h] = jnp.zeros((dim, dim), f32)

        @pl.when(takes(s, place))
        def _():
            copy(s, h).wait_recv()
            merge(h, s, place, tot, rcv, first)

        if s + 1 < stages:
            begin(copy, s + 1, h, place)

    def merge(h, s, place, tot, rcv, first):
        g = 1 << s
        r = rate(h, dim) * slab
        upper = jnp.full((1, dim), lax.rem(lax.div(place, g), 2), jnp.int32).astype(f32)
        inner = jnp.full((1, dim), lax.rem(place, g), jnp.int32).astype(f32)
        got = rcv[s, h]
        to_prefix = upper * jnp.exp2(-r * inner)
        if first:
            pref[h] = to_prefix * got
        else:
            pref[h] = pref[h] + to_prefix * got
        if s + 1 < stages:
            whole = jnp.exp2(-r * g)
            from_got = upper * whole + (1.0 - upper)
            from_own = upper + (1.0 - upper) * whole
            tot[s + 1, h] = from_got * got + from_own * tot[s, h]

    loads[0].wait()
    loads[1].wait()

    @pl.loop(0, heads)
    def _(h):
        faded = (k[:, cols(h)].astype(f32) * down[h]).astype(bf16)
        tot_f[0, h] = dot(faded, v[:, cols(h)], 0, 0)
        begin(fwd_copy, 0, h, me)

    loads[2].wait()

    t_at = lax.broadcasted_iota(jnp.int32, (blk, blk), 0)
    s_at = lax.broadcasted_iota(jnp.int32, (blk, blk), 1)

    @pl.loop(0, heads)
    def _(h):
        r = rate(h, dim)
        place = lax.broadcasted_iota(jnp.int32, (1, dim), 1).astype(f32)
        front = up[h, pl.ds(0, blk), :]
        near = jnp.concatenate(
            [front * jnp.exp2(r * (place + float(b * dim))) for b in range(blk // dim)], axis=1
        )
        wtab[h, 0] = jnp.where(t_at >= s_at, near, 0.0)
        for d in range(1, nblk):
            far = jnp.exp2(-r * float(blk * d))
            wtab[h, d] = near * jnp.concatenate([far] * (blk // dim), axis=1)
        for i in range(nblk):
            rows = pl.ds(i * blk, blk)
            for j in range(i + 1):
                past = pl.ds(j * blk, blk)
                score = dot(q[rows, cols(h)], k[past, cols(h)], 1, 1)
                probs[h, rows, past] = (score * wtab[h, i - j]).astype(bf16)
            past = pl.ds(0, (i + 1) * blk)
            out[rows, cols(h)] = dot(probs[h, rows, past], v[past, cols(h)], 1, 0)
        accept(fwd_copy, h, 0, me, tot_f, rcv_f)

    for s in range(1, stages - 1):

        @pl.loop(0, heads)
        def _(h, s=s):
            accept(fwd_copy, h, s, me, tot_f, rcv_f)

    loads[3].wait()
    for load in small[1:]:
        load.wait()

    token = mask_ref[...].astype(f32)
    at = me * slab + lax.broadcasted_iota(jnp.int32, (1, slab), 1)
    length = jnp.full((1, slab), len_ref[0], jnp.int32)
    token = token * (at < length).astype(f32) * jnp.minimum(imp_ref[...], clip_high)
    token = token * adv_ref[0] * (float(slab * n_seq) / length.astype(f32))

    squares[...] = jnp.zeros((slab, dim), f32)
    mixes[...] = jnp.zeros((slab, dim), f32)

    @pl.loop(0, heads)
    def _(h):
        if stages > 1:
            accept(fwd_copy, h, stages - 1, me, tot_f, rcv_f)
        half = pref[h].astype(bf16)
        state[h] = half
        grow = up[h] * jnp.exp2(-rate(h, dim))
        full = out[:, cols(h)] + dot(q[:, cols(h)], half, 1, 0) * grow
        out[:, cols(h)] = full
        gain = gain_ref[pl.ds(h, 1), :]
        squares[...] += full * full
        mixes[...] += c[:, cols(h)].astype(f32) * gain * full

    stat[mh, 0:1, :] = jnp.sum(squares[...].T, axis=0, keepdims=True)
    stat[mh, 1:2, :] = jnp.sum(mixes[...].T, axis=0, keepdims=True) * token
    posts = [
        pltpu.make_async_remote_copy(
            src_ref=stat.at[mh],
            dst_ref=stat.at[mh],
            send_sem=ss_sem.at[off - 1],
            recv_sem=sr_sem.at[off - 1],
            device_id={"head": lax.rem(mh + off, n_head)},
            device_id_type=MESH,
        )
        for off in range(1, n_head)
    ]
    for post in posts:
        post.start()
    settle(fwd_copy, me)
    for post in posts:
        post.wait()
    sums = stat[0]
    for i in range(1, n_head):
        sums = sums + stat[i]
    count = features * n_head
    inverse = lax.rsqrt(sums[0:1] / count + epsilon)
    mean = inverse * (sums[1:2] / count)

    def column(row):
        return jnp.broadcast_to(row, (dim, slab)).T

    back = n_seq - 1 - me
    inv_col = column(inverse)
    give_col = column(inverse * token)
    take_col = column(inverse * inverse * mean)

    @pl.loop(0, heads)
    def _(h):
        gain = gain_ref[pl.ds(h, 1), :]
        full = out[:, cols(h)]
        given = c[:, cols(h)].astype(f32) * give_col
        o_mix[0, :, cols(h)] = (full * inv_col * gain).astype(bf16)
        gsum[0, pl.ds(h, 1), :] = jnp.sum(given * full, axis=0, keepdims=True)
        grad = (given * gain - take_col * full).astype(bf16)
        go[:, cols(h)] = grad
        faded = (q[:, cols(h)].astype(f32) * up[h]).astype(bf16)
        tot_b[0, h] = dot(faded, grad, 0, 0)
        begin(bwd_copy, 0, h, back)

    def gain_copy(s):
        target = {"dp": lax.rem(md + 1, n_dp)} if s == stages else {"seq": partner(s)}
        return pltpu.make_async_remote_copy(
            src_ref=gsum.at[s],
            dst_ref=grcv.at[s],
            send_sem=gs_sem.at[s],
            recv_sem=gr_sem.at[s],
            device_id=target,
            device_id_type=MESH,
        )

    gain_copy(0).start()

    @pl.loop(0, heads)
    def _(h):
        for i in range(nblk):
            rows = pl.ds(i * blk, blk)
            grad = go[rows, cols(h)]
            for j in range(i + 1):
                past = pl.ds(j * blk, blk)
                score = dot(grad, v[past, cols(h)], 1, 1)
                dsc[rows, past] = (score * wtab[h, i - j]).astype(bf16)
            past = pl.ds(0, (i + 1) * blk)
            grow = up[h, rows, :] * jnp.exp2(-rate(h, dim))
            total = dot(dsc[rows, past], k[past, cols(h)], 1, 0)
            total = total + dot(grad, state[h], 1, 1) * grow
            o_dq[0, rows, cols(h)] = total.astype(bf16)
        for j in range(nblk):
            past = pl.ds(j * blk, blk)
            rest = pl.ds(j * blk, slab - j * blk)
            pk[past, cols(h)] = dot(dsc[rest, past], q[rest, cols(h)], 0, 0)
            pv[past, cols(h)] = dot(probs[h, rest, past], go[rest, cols(h)], 0, 0)
        accept(bwd_copy, h, 0, back, tot_b, rcv_b)

    rounds = stages + (1 if n_dp > 1 else 0)
    for s in range(rounds):
        gain_copy(s).wait()
        gsum[s + 1] = gsum[s] + grcv[s]
        if s + 1 < rounds:
            gain_copy(s + 1).start()
    gg_ref[...] = gsum[rounds]

    for s in range(1, stages - 1):

        @pl.loop(0, heads)
        def _(h, s=s):
            accept(bwd_copy, h, s, back, tot_b, rcv_b)

    @pl.loop(0, heads)
    def _(h):
        if stages > 1:
            accept(bwd_copy, h, stages - 1, back, tot_b, rcv_b)
        half = pref[h].astype(bf16)
        fade = down[h] * jnp.exp2(-rate(h, dim))
        dk = pk[:, cols(h)] + dot(v[:, cols(h)], half, 1, 1) * fade
        o_dk[0, :, cols(h)] = dk.astype(bf16)
        dv = pv[:, cols(h)] + dot(k[:, cols(h)], half, 1, 0) * fade
        o_dv[0, :, cols(h)] = dv.astype(bf16)

    settle(bwd_copy, back)


def writer(n, *refs):
    sem = refs[-1]
    copies = [pltpu.make_async_copy(refs[i], refs[n + i], sem.at[i]) for i in range(n)]
    for copy in copies:
        copy.start()
    for copy in copies:
        copy.wait()


def on_device(
    n_seq,
    n_head,
    n_dp,
    query_rows,
    key_rows,
    value_rows,
    norm_gain,
    cotangent,
    loss_mask,
    importance,
    advantage,
    lengths,
    decay_index,
):
    batches, slab, features = query_rows.shape
    heads = decay_index.shape[0]
    dim = features // heads
    stages = n_seq.bit_length() - 1
    assert batches == 1 and n_seq == 1 << stages and stages > 0 and n_dp <= 2
    vmem = pl.BlockSpec(memory_space=pltpu.VMEM)
    smem = pl.BlockSpec(memory_space=pltpu.SMEM)
    far = pl.BlockSpec(memory_space=pltpu.HBM)
    rows = jax.ShapeDtypeStruct(query_rows.shape, bf16)
    wide = pltpu.VMEM((slab, features), bf16)
    wide32 = pltpu.VMEM((slab, features), f32)
    blk = min(256, slab)
    states = pltpu.VMEM((stages, heads, dim, dim), f32)
    dma = pltpu.SemaphoreType.DMA

    def stay(array):
        return pltpu.with_memory_space_constraint(array, pltpu.HBM)

    results = pl.pallas_call(
        functools.partial(kernel, n_seq, n_head, n_dp),
        out_shape=(rows, rows, rows, rows, jax.ShapeDtypeStruct((heads, dim), f32)),
        in_specs=[far, smem, smem] + [far] * 7,
        out_specs=(vmem,) * 5,
        scratch_shapes=[
            pltpu.SMEM((heads,), jnp.int32),
            pltpu.VMEM((heads, dim), f32),
            pltpu.VMEM((1, slab), jnp.int32),
            pltpu.VMEM((1, slab), f32),
        ]
        + [wide] * 4
        + [wide32, wide, wide32, wide32]
        + [
            pltpu.VMEM((heads, slab, slab), bf16),
            pltpu.VMEM((slab, slab), bf16),
            pltpu.VMEM((heads, slab // blk, blk, blk), f32),
            pltpu.VMEM((heads, slab, dim), f32),
            pltpu.VMEM((heads, slab, dim), f32),
            pltpu.VMEM((slab, dim), f32),
            pltpu.VMEM((slab, dim), f32),
            states,
            states,
            states,
            states,
            pltpu.VMEM((heads, dim, dim), f32),
            pltpu.VMEM((heads, dim, dim), bf16),
            pltpu.VMEM((n_head, 2, slab), f32),
            pltpu.VMEM((stages + 2, heads, dim), f32),
            pltpu.VMEM((stages + 1, heads, dim), f32),
            dma((4,)),
            dma((4,)),
            dma((stages, heads)),
            dma((stages, heads)),
            dma((stages, heads)),
            dma((stages, heads)),
            dma((max(n_head - 1, 1),)),
            dma((max(n_head - 1, 1),)),
            dma((stages + 1,)),
            dma((stages + 1,)),
        ],
        compiler_params=pltpu.CompilerParams(
            collective_id=0, has_side_effects=True, vmem_limit_bytes=48 << 20
        ),
        name="lightning",
    )(
        stay(decay_index),
        advantage,
        lengths,
        stay(norm_gain.reshape(heads, dim)),
        stay(loss_mask),
        stay(importance),
        stay(query_rows),
        stay(key_rows),
        stay(value_rows),
        stay(cotangent),
    )
    shapes = tuple(jax.ShapeDtypeStruct(r.shape, r.dtype) for r in results)
    any_space = pl.BlockSpec(memory_space=pl.ANY)
    mixed, dq, dk, dv, gain_grad = pl.pallas_call(
        functools.partial(writer, len(shapes)),
        out_shape=shapes,
        in_specs=[vmem] * len(shapes),
        out_specs=(any_space,) * len(shapes),
        scratch_shapes=[dma((len(shapes),))],
        compiler_params=pltpu.CompilerParams(vmem_limit_bytes=8 << 20),
        name="writer",
    )(*results)
    return (mixed, dq, dk, dv, gain_grad.reshape(features))


def solution(mesh):
    wide = P("dp", "seq", "head")
    token = P("dp", "seq")
    in_specs = (wide, wide, wide, P("head"), wide, token, token, P("dp"), P("dp"), P("head"))
    out_specs = (wide, wide, wide, wide, P("head"))
    body = functools.partial(on_device, mesh.shape["seq"], mesh.shape["head"], mesh.shape["dp"])
    return jax.shard_map(
        body, mesh=mesh, in_specs=in_specs, out_specs=out_specs, check_vma=False
    )
```
